32 devices in a mesh: dp: 16 (over z, y, x), mp: 2 (over core).
Axes of the slice: x: 2, y: 2, z: 4, core: 2. Of those that a mesh axis runs over, the one named last changes fastest.
Arguments:
- tokens: bfloat16 [32, 768, 1024], P(('dp', 'mp')), may hold values from -6 to 6
- cotangent: bfloat16 [32, 768, 1024], P(('dp', 'mp')), may hold values from -6 to 6
- class_ids: int32 [32], replicated, may hold values from 0 to 1000
- stop_scales: int32 [32], replicated, may hold values from 7 to 10, as said below
- qkv_weight: bfloat16 [1024, 3, 1024], P(None, None, 'mp'), may hold values from -0.1875 to 0.1875
- query_bias: float32 [1024], P('mp'), may hold values from -3 to 3
- value_bias: float32 [1024], P('mp'), may hold values from -3 to 3
- head_scale: float32 [16], P('mp'), may hold values from 2 to 3
- proj_weight: bfloat16 [1024, 1024], P(None, 'mp'), may hold values from -0.75 to 0.75
- proj_bias: float32 [1024], replicated, may hold values from -1.75 to 1.75
- up_weight: bfloat16 [1024, 4096], P(None, 'mp'), may hold values from -0.1875 to 0.1875
- up_bias: float32 [4096], P('mp'), may hold values from -1.75 to 1.75
- down_weight: bfloat16 [1024, 4096], P(None, 'mp'), may hold values from -0.1875 to 0.1875
- down_bias: float32 [1024], replicated, may hold values from -1.75 to 1.75
- ada_weight: bfloat16 [1024, 6, 1024], replicated, may hold values from -0.1875 to 0.1875
- ada_bias: float32 [1024, 6], replicated, may hold values from -1.75 to 1.75
- class_table: bfloat16 [1024, 1001], replicated, may hold values from -6 to 6
Outputs:
- output: bfloat16 [32, 768, 1024], P(('dp', 'mp'))
- gradient_of_input: bfloat16 [32, 768, 1024], P(('dp', 'mp'))
- qkv_grad: float32 [1024, 3, 1024], P('dp', None, 'mp')
- query_bias_grad: float32 [1024], P('mp')
- value_bias_grad: float32 [1024], P('mp')
- head_scale_grad: float32 [16], P('mp')
- proj_grad: float32 [1024, 1024], P('dp', 'mp')
- proj_bias_grad: float32 [1024], P('dp')
- up_grad: float32 [1024, 4096], P('dp', 'mp')
- up_bias_grad: float32 [4096], P('mp')
- down_grad: float32 [1024, 4096], P('dp', 'mp')
- down_bias_grad: float32 [1024], P('dp')
- ada_grad: float32 [1024, 6, 1024], P('dp')
- ada_bias_grad: float32 [1024, 6], P('dp')
- table_grad: float32 [1024, 1001], P('dp')
The draws below stay inside these ranges and needn't reach their ends.
Inputs may be any that keep to these rules, and one draw needn't show every extreme that they name: `stop_scales`: each item uses 10 - 3 to 10 token maps, and some item uses all 10.
All inputs are finite; a program needn't handle non-finite values.
Results may differ from the reference program's by a relative error of at most 0.018.
Values may be sent and summed in bfloat16 or wider, within the bound.
No kernel may reach another device: no remote copies, remote signals or barrier semaphores. Data moves between devices by JAX's collectives and lax.ppermute only.
A program may use at most 256 MiB of HBM per device.

```python
import jax
import jax.numpy as jnp
import numpy as np
from jax import lax

D = 1024
HEADS = 16
FF = 4096
CLASSES = 1001
SCALES = 10
L_PAD = 768
ITEMS = 32


def draw_stop_scales(key, part):
    first_key, second_key = jax.random.split(jax.random.fold_in(key, 17))
    stop_values = jax.random.randint(first_key, (ITEMS,), SCALES - 3, SCALES + 1)
    chosen = jax.random.randint(second_key, (), 0, ITEMS)
    return jnp.where(jnp.arange(ITEMS) == chosen, SCALES, stop_values).astype(jnp.int32)


def with_ends(result, key, smallest, high):
    index_at = [jax.random.randint(jax.random.fold_in(key, axis), (), 0, length) for axis, length in enumerate(result.shape)]
    main_axis = result.shape.index(max(result.shape))
    neighbour = index_at[:main_axis] + [(index_at[main_axis] + 1) % result.shape[main_axis]] + index_at[main_axis + 1:]
    return result.at[tuple(index_at)].set(smallest).at[tuple(neighbour)].set(high)


def strengthened(result, rng, source, target, parts, factor):
    owner, partner = [(jnp.arange(result.shape[axis_at]) // (result.shape[axis_at] // parts)).reshape([-1 if axis == axis_at else 1 for axis in range(result.ndim)]) for axis_at in (source, target)]
    chosen = jax.random.permutation(rng, parts)[partner]
    strong = (owner == chosen) | (owner == (partner + parts // 2) % parts)
    return jnp.where(strong, factor * result, result)


def block_scale(rng, extent, cuts, least, high):
    factor_of = 1.0
    for axis_at, blocks in cuts:
        heights = jax.random.uniform(jax.random.fold_in(jax.random.fold_in(rng, 6), axis_at), (blocks,), jnp.float32, least / len(cuts), high / len(cuts))
        factor_of = factor_of * jnp.repeat(jnp.exp(heights), extent[axis_at] // blocks).reshape((-1,) + (1,) * (len(extent) - 1 - axis_at))
    return factor_of


def gaussian(rng, extent, width, most, cuts=(), kind=jnp.bfloat16):
    values = width * jax.random.normal(rng, extent, jnp.float32)
    if cuts:
        values = values * block_scale(rng, extent, cuts, -0.22, 0.18)
    return jnp.clip(values, -most, most).astype(kind)


def heavy_noise(rng, extent, scale, most, cuts, heavy, kind=jnp.bfloat16):
    drawn = scale * jax.random.normal(rng, extent, jnp.float32)
    if cuts:
        drawn = drawn * block_scale(rng, extent, cuts, -0.22, 0.18)
    return jnp.clip(strengthened(drawn, jax.random.fold_in(rng, 3), *heavy), -most, most).astype(kind)


def setup_inputs(seed: int = 0) -> dict:
    splits = jax.random.split(jax.random.key(seed), 18)
    tokens = gaussian(splits[0], (ITEMS, L_PAD, D), 1.0, 6.0, ((0, 32),))
    cotangent = heavy_noise(splits[1], (ITEMS, L_PAD, D), 1.0, 6.0, ((0, 32),), (0, 2, 32, 2.75))
    class_ids = with_ends(jax.random.randint(splits[2], (ITEMS,), 0, CLASSES), jax.random.fold_in(splits[2], 1), 0, CLASSES - 1).astype(jnp.int32)
    stop_scales = draw_stop_scales(jax.random.fold_in(splits[17], 71), 0)
    qkv_weight = gaussian(splits[4], (D, 3, D), D ** -0.5, 0.1875, ((2, 2),))
    query_bias = gaussian(splits[5], (D,), 0.5, 3.0, ((0, 2),), jnp.float32)
    value_bias = gaussian(splits[6], (D,), 0.5, 3.0, ((0, 2),), jnp.float32)
    head_scale = jnp.clip(2.0 + 1.0 * jax.random.uniform(splits[7], (HEADS,), jnp.float32) ** block_scale(splits[7], (HEADS,), ((0, 2),), -0.2, 0.2), 2.0, 3.0)
    proj_weight = gaussian(splits[8], (D, D), (D // 16) ** -0.5, 0.75, ((1, 2),))
    proj_bias = gaussian(splits[9], (D,), 0.3, 1.75, (), jnp.float32)
    up_weight = gaussian(splits[10], (D, FF), D ** -0.5, 0.1875, ((1, 2),))
    up_bias = gaussian(splits[11], (FF,), 0.3, 1.75, ((0, 2),), jnp.float32)
    down_weight = gaussian(splits[12], (D, FF), (FF // 4) ** -0.5, 0.1875, ((1, 2),))
    down_bias = gaussian(splits[13], (D,), 0.3, 1.75, (), jnp.float32)
    ada_weight = gaussian(splits[14], (D, 6, D), D ** -0.5, 0.1875)
    ada_bias = gaussian(splits[15], (D, 6), 0.3, 1.75, (), jnp.float32)
    class_table = gaussian(splits[16], (D, CLASSES), 1.0, 6.0)
    return dict(tokens=tokens, cotangent=cotangent, class_ids=class_ids, stop_scales=stop_scales, qkv_weight=qkv_weight, query_bias=query_bias, value_bias=value_bias, head_scale=head_scale, proj_weight=proj_weight, proj_bias=proj_bias, up_weight=up_weight, up_bias=up_bias, down_weight=down_weight, down_bias=down_bias, ada_weight=ada_weight, ada_bias=ada_bias, class_table=class_table)


side_list = (1, 2, 3, 4, 5, 6, 8, 10, 13, 16)
norm_eps = 1e-06
unit_eps = 1e-06
masked_score = -1e+30
highest = lax.Precision.HIGHEST

@jax.custom_vjp
def low(v):
    return lax.optimization_barrier(v.astype(jnp.bfloat16)).astype(jnp.float32)

@jax.custom_vjp
def low_back(v):
    return v

def low_keep(v):
    return (low(v), None)

def low_pass(kept, grad):
    return (grad,)

def back_keep(v):
    return (v, None)

def back_low(kept, grad):
    return (low(grad),)
low.defvjp(low_keep, low_pass)
low_back.defvjp(back_keep, back_low)

def scale_limits():
    side_array = np.array(side_list[:SCALES], dtype=np.int64)
    return [int(limit) for limit in np.cumsum(side_array * side_array)]

def scale_number(positions):
    counted = jnp.zeros(positions.shape, jnp.int32)
    for limit in scale_limits():
        counted = counted + (positions >= limit).astype(jnp.int32)
    return counted

def item_lengths(stop_values):
    limits = jnp.array(scale_limits(), dtype=jnp.int32)
    chosen = jnp.arange(SCALES, dtype=jnp.int32)[None, :] == stop_values[:, None] - 1
    return lax.optimization_barrier(jnp.sum(jnp.where(chosen, limits[None, :], 0), axis=1)).astype(jnp.int32)

def allowed_mask(row_count, length):
    positions = jnp.arange(row_count, dtype=jnp.int32)
    scales = scale_number(positions)
    return (scales[None, :] <= scales[:, None]) & (positions[None, :] < length)

def norm_rows(values):
    centered = values - lax.optimization_barrier(jnp.mean(values, axis=-1, keepdims=True))
    spread = lax.optimization_barrier(jnp.mean(centered * centered, axis=-1, keepdims=True))
    return centered * lax.rsqrt(spread + norm_eps)

def unit_heads(values):
    return values * lax.rsqrt(lax.optimization_barrier(jnp.sum(values * values, axis=-1, keepdims=True)) + unit_eps)

def item_forward(params, token_rows, class_id, length):
    qkv_weight, query_bias, value_bias, head_scale, proj_weight, proj_bias, up_weight, up_bias, down_weight, down_bias, ada_weight, ada_bias, class_table = params
    row_count = token_rows.shape[0]
    head_count = head_scale.shape[0]
    cond = lax.dynamic_slice_in_dim(class_table, class_id.astype(jnp.int32), 1, 1)[:, 0]
    raised_values = low(jax.nn.silu(cond))
    modulation = jnp.einsum('i,iko->ko', raised_values, ada_weight, precision=highest) + ada_bias.T
    first = low_back(low(norm_rows(token_rows) * (1.0 + modulation[2]) + modulation[4]))
    projected = jnp.einsum('ld,dko->lko', first, qkv_weight, precision=highest)
    query_raw = low_back(projected[:, 0] + query_bias).reshape(row_count, head_count, -1)
    keys_raw = low_back(projected[:, 1]).reshape(row_count, head_count, -1)
    values = low_back(low(projected[:, 2] + value_bias)).reshape(row_count, head_count, -1)
    query_low = low(unit_heads(query_raw) * jnp.exp(head_scale)[None, :, None])
    keys_low = low(unit_heads(keys_raw))
    scores = low_back(jnp.einsum('qhd,khd->hqk', query_low, keys_low, precision=highest))
    scores = jnp.where(allowed_mask(row_count, length)[None], scores, masked_score)
    largest = lax.optimization_barrier(jnp.max(scores, axis=2, keepdims=True))
    exponent = jnp.exp(scores - largest)
    softmax_low = low(exponent / lax.optimization_barrier(jnp.sum(exponent, axis=2, keepdims=True)))
    joined = jnp.einsum('hqk,khd->qhd', softmax_low, values, precision=highest)
    joined = low_back(low(joined.reshape(row_count, -1)))
    branch = jnp.einsum('lj,oj->lo', joined, proj_weight, precision=highest) + proj_bias
    branch = low_back(low(branch))
    middle = token_rows + modulation[0] * branch
    second = low(norm_rows(middle) * (1.0 + modulation[3]) + modulation[5])
    pre = low_back(jnp.einsum('ld,df->lf', second, up_weight, precision=highest) + up_bias)
    hidden = low(jax.nn.gelu(pre, approximate=True))
    mlp_out = low_back(jnp.einsum('lf,of->lo', hidden, down_weight, precision=highest) + down_bias)
    return middle + modulation[1] * mlp_out

def reference(tokens, cotangent, class_ids, stop_scales, qkv_weight, query_bias, value_bias, head_scale, proj_weight, proj_bias, up_weight, up_bias, down_weight, down_bias, ada_weight, ada_bias, class_table):
    params = tuple((array.astype(jnp.float32) for array in (qkv_weight, query_bias, value_bias, head_scale, proj_weight, proj_bias, up_weight, up_bias, down_weight, down_bias, ada_weight, ada_bias, class_table)))
    tokens_wide = tokens.astype(jnp.float32)
    lengths = item_lengths(stop_scales)
    positions = jnp.arange(tokens.shape[1], dtype=jnp.int32)
    live = (positions[None, :] < lengths[:, None]).astype(jnp.float32)
    grad_out = cotangent.astype(jnp.float32) * live[:, :, None]

    def whole(token_all, param_all):
        stepper = jax.checkpoint(item_forward)

        def one_item(packed):
            return stepper(param_all, packed[0], packed[1], packed[2])
        return lax.map(one_item, (token_all, class_ids, lengths))
    output, back = jax.vjp(whole, tokens_wide, params)
    gradient_of_input, grads = back(grad_out)
    return (output.astype(jnp.bfloat16), gradient_of_input.astype(jnp.bfloat16), grads[0], grads[1], grads[2], grads[3], grads[4], grads[5], grads[6], grads[7], grads[8], grads[9], grads[10], grads[11], grads[12])
```

```python
import jax
import jax.numpy as jnp
import numpy as np
from jax import lax
from jax.sharding import PartitionSpec as P

SCALES = 10
side_list = (1, 2, 3, 4, 5, 6, 8, 10, 13, 16)
norm_eps = 1e-06
unit_eps = 1e-06
masked_score = -1e30
highest = lax.Precision.HIGHEST
bf16 = jnp.bfloat16
f32 = jnp.float32


def scale_limits():
    side_array = np.array(side_list[:SCALES], dtype=np.int64)
    return [int(limit) for limit in np.cumsum(side_array * side_array)]


def scale_number(positions):
    counted = jnp.zeros(positions.shape, jnp.int32)
    for limit in scale_limits():
        counted = counted + (positions >= limit).astype(jnp.int32)
    return counted


def item_lengths(stop_values):
    limits = jnp.array(scale_limits(), dtype=jnp.int32)
    chosen = jnp.arange(SCALES, dtype=jnp.int32)[None, :] == stop_values[:, None] - 1
    return jnp.sum(jnp.where(chosen, limits[None, :], 0), axis=1)


def allowed_mask(row_count, length):
    positions = jnp.arange(row_count, dtype=jnp.int32)
    scales = scale_number(positions)
    return (scales[None, :] <= scales[:, None]) & (positions[None, :] < length)


def norm_rows(values):
    centered = values - jnp.mean(values, axis=-1, keepdims=True)
    spread = jnp.mean(centered * centered, axis=-1, keepdims=True)
    inverse = lax.rsqrt(spread + norm_eps)
    return centered * inverse, inverse


def norm_back(grad, scaling, normal, inverse):
    scaled = grad * (1.0 + scaling)
    return inverse * (
        scaled
        - jnp.mean(scaled, axis=-1, keepdims=True)
        - normal * jnp.mean(scaled * normal, axis=-1, keepdims=True)
    )


def unit_heads(values):
    return values * lax.rsqrt(jnp.sum(values * values, axis=-1, keepdims=True) + unit_eps)


def gelu_tanh(values):
    return jax.nn.gelu(values, approximate=True)


def normalize_pair(query_raw, keys_raw, head_scale):
    return (unit_heads(query_raw) * jnp.exp(head_scale)[None, :, None], unit_heads(keys_raw))


def dot(left, right, left_axis, right_axis):
    return lax.dot_general(
        left, right, (((left_axis,), (right_axis,)), ((), ())), preferred_element_type=f32
    )


def swap_pair(values):
    return lax.ppermute(values, "mp", [(0, 1), (1, 0)])


def attention_front(query_raw, keys_raw, values, head_scale, length):
    rows = query_raw.shape[0]
    heads = head_scale.shape[0]
    query_raw = query_raw.reshape(rows, heads, -1)
    keys_raw = keys_raw.reshape(rows, heads, -1)
    values = values.reshape(rows, heads, -1)
    query_low = (unit_heads(query_raw) * jnp.exp(head_scale)[None, :, None]).astype(bf16)
    keys_low = unit_heads(keys_raw).astype(bf16)
    scores = jnp.einsum("qhd,khd->hqk", query_low, keys_low, preferred_element_type=f32)
    scores = jnp.where(allowed_mask(rows, length)[None], scores, masked_score)
    largest = jnp.max(scores, axis=2, keepdims=True)
    exponent = jnp.exp(scores - largest)
    row_sum = jnp.sum(exponent, axis=2, keepdims=True)
    softmax_low = (exponent / row_sum).astype(bf16)
    joined = jnp.einsum("hqk,khd->qhd", softmax_low, values, preferred_element_type=f32)
    return joined.reshape(rows, -1).astype(bf16), largest + jnp.log(row_sum)


def attention_back(grad_joined, query_raw, keys_raw, values, log_total, head_scale, length):
    rows = query_raw.shape[0]
    heads = head_scale.shape[0]
    grad_joined = grad_joined.reshape(rows, heads, -1)
    query_raw = query_raw.reshape(rows, heads, -1)
    keys_raw = keys_raw.reshape(rows, heads, -1)
    values = values.reshape(rows, heads, -1)
    unit_pair, normalize_backward = jax.vjp(normalize_pair, query_raw, keys_raw, head_scale)
    query_low = unit_pair[0].astype(bf16)
    keys_low = unit_pair[1].astype(bf16)
    scores = jnp.einsum("qhd,khd->hqk", query_low, keys_low, preferred_element_type=f32)
    scores = jnp.where(allowed_mask(rows, length)[None], scores, masked_score)
    softmax_full = jnp.exp(scores - log_total)
    grad_soft = jnp.einsum("qhd,khd->hqk", grad_joined, values, preferred_element_type=f32)
    grad_values = jnp.einsum(
        "hqk,qhd->khd", softmax_full.astype(bf16), grad_joined, preferred_element_type=f32
    ).astype(bf16)
    inner = jnp.sum(softmax_full * grad_soft, axis=2, keepdims=True)
    grad_scores = (softmax_full * (grad_soft - inner)).astype(bf16)
    query_part = jnp.einsum("hqk,khd->qhd", grad_scores, keys_low, preferred_element_type=f32)
    key_part = jnp.einsum("hqk,qhd->khd", grad_scores, query_low, preferred_element_type=f32)
    grad_query, grad_keys, grad_scale = normalize_backward((query_part, key_part))
    return (
        grad_query.astype(bf16).reshape(rows, -1),
        grad_keys.astype(bf16).reshape(rows, -1),
        grad_values.reshape(rows, -1),
        grad_scale,
    )


def scatter_rows(values, axis):
    return lax.psum_scatter(values, "dp", scatter_dimension=axis, tiled=True)


def per_device(
    tokens,
    cotangent,
    class_ids,
    stop_scales,
    qkv_weight,
    query_bias,
    value_bias,
    head_scale,
    proj_weight,
    proj_bias,
    up_weight,
    up_bias,
    down_weight,
    down_bias,
    ada_weight,
    ada_bias,
    class_table,
):
    pair_count = lax.axis_size("mp")
    data_count = lax.axis_size("dp")
    pair_index = lax.axis_index("mp")
    data_index = lax.axis_index("dp")
    slots, width = tokens.shape[1:]
    items = class_ids.shape[0]
    classes = class_table.shape[1]
    own_rows = width // data_count
    row_first = data_index * own_rows
    own = data_index * pair_count + pair_index
    half_heads = head_scale.shape[0]
    half_width = query_bias.shape[0]
    half_units = up_bias.shape[0]

    qkv_own = jnp.transpose(qkv_weight, (1, 0, 2))
    attn_own = jnp.concatenate([qkv_own, proj_weight[None]], axis=0)
    attn_other = swap_pair(attn_own)
    small_own = jnp.concatenate([query_bias, value_bias, up_bias, head_scale])
    small_other = swap_pair(small_own)
    up_other = swap_pair(up_weight)
    down_other = swap_pair(down_weight)
    cuts = np.cumsum([half_width, half_width, half_units]).tolist()
    query_bias_other, value_bias_other, up_bias_other, head_scale_other = jnp.split(
        small_other, cuts
    )
    attn_halves = (
        (qkv_own, proj_weight, query_bias, value_bias, head_scale),
        (attn_other[:3], attn_other[3], query_bias_other, value_bias_other, head_scale_other),
    )
    unit_halves = (
        (up_weight, up_bias, down_weight),
        (up_other, up_bias_other, down_other),
    )

    lengths = item_lengths(stop_scales)
    length = jnp.sum(jnp.where(jnp.arange(items, dtype=jnp.int32) == own, lengths, 0))
    class_hot = (class_ids[:, None] == jnp.arange(classes, dtype=jnp.int32)[None, :]).astype(bf16)
    cond_all = jnp.einsum("bc,dc->bd", class_hot, class_table, preferred_element_type=f32)
    lifted_all = jax.nn.silu(cond_all).astype(bf16)
    lifted_own = lax.dynamic_slice_in_dim(lifted_all, own, 1, 0)
    modulation = (
        jnp.einsum("bi,iko->bko", lifted_own, ada_weight, preferred_element_type=f32)[0]
        + ada_bias.T
    )
    gamma_one, gamma_two, scale_one, scale_two, shift_one, shift_two = [
        modulation[k : k + 1] for k in range(6)
    ]

    tokens_wide = tokens[0].astype(f32)
    normal_one, inverse_one = norm_rows(tokens_wide)
    first = (normal_one * (1.0 + scale_one) + shift_one).astype(bf16)
    attn_saved = []
    branch = proj_bias[None]
    for qkv_half, proj_half, qb, vb, hs in attn_halves:
        query_raw = dot(first, qkv_half[0], 1, 0) + qb
        keys_raw = dot(first, qkv_half[1], 1, 0)
        values = (dot(first, qkv_half[2], 1, 0) + vb).astype(bf16)
        joined, log_total = attention_front(query_raw, keys_raw, values, hs, length)
        attn_saved.append((query_raw, keys_raw, values, joined, log_total))
        branch = branch + dot(joined, proj_half, 1, 1)
    branch = branch.astype(bf16)
    middle = tokens_wide + gamma_one * branch.astype(f32)
    normal_two, inverse_two = norm_rows(middle)
    second = (normal_two * (1.0 + scale_two) + shift_two).astype(bf16)
    unit_saved = []
    mlp_out = down_bias[None]
    for up_half, ub, down_half in unit_halves:
        pre = dot(second, up_half, 1, 0) + ub
        hidden = gelu_tanh(pre).astype(bf16)
        unit_saved.append((pre, hidden))
        mlp_out = mlp_out + dot(hidden, down_half, 1, 1)
    output = (middle + gamma_two * mlp_out).astype(bf16)

    live = (jnp.arange(slots, dtype=jnp.int32) < length).astype(f32)
    grad_out = cotangent[0].astype(f32) * live[:, None]
    grad_gamma_two = jnp.sum(grad_out * mlp_out, axis=0)
    grad_mlp = (grad_out * gamma_two).astype(bf16)
    down_bias_part = jnp.sum(grad_mlp.astype(f32), axis=0)
    grad_pres = []
    grad_second = None
    for (up_half, ub, down_half), (pre, hidden) in zip(unit_halves, unit_saved):
        grad_hidden = dot(grad_mlp, down_half, 1, 0)
        grad_pre = jax.vjp(gelu_tanh, pre)[1](grad_hidden)[0].astype(bf16)
        grad_pres.append(grad_pre)
        part = dot(grad_pre, up_half, 1, 1)
        grad_second = part if grad_second is None else grad_second + part
    up_bias_parts = [jnp.sum(g.astype(f32), axis=0) for g in grad_pres]
    down_got = swap_pair(dot(grad_mlp, unit_saved[1][1], 0, 0).astype(bf16))
    down_part = (dot(grad_mlp, unit_saved[0][1], 0, 0) + down_got.astype(f32)).astype(bf16)
    down_grad = scatter_rows(down_part, 0).astype(f32)
    up_got = swap_pair(dot(second, grad_pres[1], 0, 0).astype(bf16))
    up_part = (dot(second, grad_pres[0], 0, 0) + up_got.astype(f32)).astype(bf16)
    up_grad = scatter_rows(up_part, 0).astype(f32)

    grad_scale_two = jnp.sum(grad_second * normal_two, axis=0)
    grad_shift_two = jnp.sum(grad_second, axis=0)
    grad_middle = grad_out + norm_back(grad_second, scale_two, normal_two, inverse_two)
    grad_gamma_one = jnp.sum(grad_middle * branch.astype(f32), axis=0)
    grad_branch = (grad_middle * gamma_one).astype(bf16)
    proj_bias_part = jnp.sum(grad_branch.astype(f32), axis=0)
    proj_got = swap_pair(dot(grad_branch, attn_saved[1][3], 0, 0).astype(bf16))
    proj_part = (dot(grad_branch, attn_saved[0][3], 0, 0) + proj_got.astype(f32)).astype(bf16)
    proj_grad = scatter_rows(proj_part, 0).astype(f32)

    def ordered(parts):
        lower = jnp.where(pair_index == 0, parts[0], parts[1])
        upper = jnp.where(pair_index == 0, parts[1], parts[0])
        return jnp.concatenate([lower, upper])

    def gather_items(vectors):
        packed = jnp.concatenate(vectors)
        count = packed.shape[0]
        padded = -(-count // 1024) * 1024
        packed = jnp.pad(packed, (0, padded - count)).reshape(1, padded // 128, 128)
        gathered = lax.all_gather(packed, ("dp", "mp"), axis=0, tiled=True)
        return gathered.reshape(items, padded)

    early = gather_items(
        [
            grad_gamma_one,
            grad_gamma_two,
            grad_scale_two,
            grad_shift_two,
            down_bias_part,
            proj_bias_part,
            ordered(up_bias_parts),
        ]
    )

    back = []
    grad_first = None
    for (qkv_half, proj_half, qb, vb, hs), (query_raw, keys_raw, values, joined, log_total) in zip(
        attn_halves, attn_saved
    ):
        grad_joined = dot(grad_branch, proj_half, 1, 0).astype(bf16)
        grads = attention_back(grad_joined, query_raw, keys_raw, values, log_total, hs, length)
        back.append(grads)
        for kind in range(3):
            part = dot(grads[kind], qkv_half[kind], 1, 1)
            grad_first = part if grad_first is None else grad_first + part
    qkv_sent = jnp.stack([dot(first, back[1][kind], 0, 0).astype(bf16) for kind in range(3)])
    qkv_got = swap_pair(qkv_sent)
    qkv_part = jnp.stack(
        [
            (dot(first, back[0][kind], 0, 0) + qkv_got[kind].astype(f32)).astype(bf16)
            for kind in range(3)
        ]
    )
    qkv_grad = jnp.transpose(scatter_rows(qkv_part, 1), (1, 0, 2)).astype(f32)
    grad_first = grad_first.astype(bf16).astype(f32)
    grad_scale_one = jnp.sum(grad_first * normal_one, axis=0)
    grad_shift_one = jnp.sum(grad_first, axis=0)
    gradient_of_input = (
        grad_middle + norm_back(grad_first, scale_one, normal_one, inverse_one)
    ).astype(bf16)
    late = gather_items(
        [
            grad_scale_one,
            grad_shift_one,
            ordered([jnp.sum(b[0].astype(f32), axis=0) for b in back]),
            ordered([jnp.sum(b[2].astype(f32), axis=0) for b in back]),
            ordered([b[3] for b in back]),
        ]
    )

    early_sum = jnp.sum(early[:, 4 * width :], axis=0)
    late_sum = jnp.sum(late[:, 2 * width :], axis=0)

    def pair_slice(values, amount):
        return lax.dynamic_slice_in_dim(values, pair_index * amount, amount, 0)

    def data_slice(values):
        return lax.dynamic_slice_in_dim(values, row_first, own_rows, 0)

    down_bias_grad = data_slice(early_sum[:width])
    proj_bias_grad = data_slice(early_sum[width : 2 * width])
    up_bias_grad = pair_slice(early_sum[2 * width : 2 * width + 2 * half_units], half_units)
    query_bias_grad = pair_slice(late_sum[:width], half_width)
    value_bias_grad = pair_slice(late_sum[width : 2 * width], half_width)
    head_scale_grad = pair_slice(late_sum[2 * width : 2 * width + 2 * half_heads], half_heads)
    grad_mod = jnp.stack(
        [
            early[:, :width],
            early[:, width : 2 * width],
            late[:, :width],
            early[:, 2 * width : 3 * width],
            late[:, width : 2 * width],
            early[:, 3 * width : 4 * width],
        ],
        axis=1,
    )
    lifted_rows = lax.dynamic_slice_in_dim(lifted_all, row_first, own_rows, 1).astype(f32)
    cond_rows = lax.dynamic_slice_in_dim(cond_all, row_first, own_rows, 1)
    ada_rows = lax.dynamic_slice_in_dim(ada_weight, row_first, own_rows, 0).astype(f32)
    ada_grad = jnp.einsum(
        "bi,bko->iko", lifted_rows, grad_mod, precision=highest, preferred_element_type=f32
    )
    ada_bias_grad = lax.dynamic_slice_in_dim(jnp.sum(grad_mod, axis=0), row_first, own_rows, 1).T
    grad_lifted = jnp.einsum(
        "bko,iko->bi", grad_mod, ada_rows, precision=highest, preferred_element_type=f32
    )
    grad_cond = jax.vjp(jax.nn.silu, cond_rows)[1](grad_lifted)[0]
    table_grad = jnp.einsum(
        "bd,bc->dc",
        grad_cond,
        class_hot.astype(f32),
        precision=highest,
        preferred_element_type=f32,
    )
    return (
        output[None],
        gradient_of_input[None],
        qkv_grad,
        query_bias_grad,
        value_bias_grad,
        head_scale_grad,
        proj_grad,
        proj_bias_grad,
        up_grad,
        up_bias_grad,
        down_grad,
        down_bias_grad,
        ada_grad,
        ada_bias_grad,
        table_grad,
    )


def solution(mesh):
    return jax.shard_map(
        per_device,
        mesh=mesh,
        in_specs=(
            P(("dp", "mp"), None, None),
            P(("dp", "mp"), None, None),
            P(),
            P(),
            P(None, None, "mp"),
            P("mp"),
            P("mp"),
            P("mp"),
            P(None, "mp"),
            P(),
            P(None, "mp"),
            P("mp"),
            P(None, "mp"),
            P(),
            P(),
            P(),
            P(),
        ),
        out_specs=(
            P(("dp", "mp"), None, None),
            P(("dp", "mp"), None, None),
            P("dp", None, "mp"),
            P("mp"),
            P("mp"),
            P("mp"),
            P("dp", "mp"),
            P("dp"),
            P("dp", "mp"),
            P("mp"),
            P("dp", "mp"),
            P("dp"),
            P("dp", None, None),
            P("dp", None),
            P("dp", None),
        ),
        check_vma=False,
    )
```
